512 devices in a mesh: dom: 64 (over x, z_lo, core), feat: 8 (over z_hi, y).
Axes of the slice: x: 4, y: 4, z: 16 (z_hi: 2, z_lo: 8; z = z_hi * 8 + z_lo), core: 2. Of those that a mesh axis runs over, the one named last changes fastest.
Arguments:
- fine_latent: bfloat16 [256, 1048576], P('feat', 'dom'), may hold values from -6 to 6
- coarse_latent: bfloat16 [256, 524288], P('feat', 'dom'), may hold values from -6 to 6
- parents: int32 [4, 1048576], P(None, 'dom'), may hold values from 0 to 24575, as said below
- interp_weights: float32 [4, 1048576], P(None, 'dom'), may hold values from 0.1 to 1
- live_rows: int32 [64], P('dom'), may hold values from 8192 to 16384, as said below
- w_fine: bfloat16 [256, 256], replicated, may hold values from -0.25 to 0.25
- w_parent: bfloat16 [256, 256], replicated, may hold values from -0.25 to 0.25
- w_edge_out: bfloat16 [256, 256], replicated, may hold values from -0.375 to 0.375
- w_node_fine: bfloat16 [256, 256], replicated, may hold values from -0.25 to 0.25
- w_node_agg: bfloat16 [256, 256], replicated, may hold values from -0.25 to 0.25
- w_node_out: bfloat16 [256, 256], replicated, may hold values from -0.375 to 0.375
- edge_bias: float32 [256], replicated, may hold values from -3 to 3
- node_bias: float32 [256], replicated, may hold values from -3 to 3
- norm_gain: float32 [256], replicated, may hold values from 0.1 to 1.9
- norm_bias: float32 [256], replicated, may hold values from -2 to 2
Outputs:
- fine_out: bfloat16 [256, 1048576], P('feat', 'dom')
The draws below stay inside these ranges and needn't reach their ends.
Inputs may be any that keep to these rules, and one draw needn't show every extreme that they name: `parents`: a parent slot s of a fine node of block b names coarse node (b - 1) * 8192 + s, block b holding coarse nodes b * 8192 to (b + 1) * 8192 - 1; slots of block 0 are at least 8192, slots of the last block under 2 * 8192. `live_rows`: fine node slots of a block at or beyond its count are padding; at least one block is full.
All inputs are finite; a program needn't handle non-finite values.
Results may differ from the reference program's by a relative error of at most 0.0042.
Values may be sent and summed in bfloat16 or wider, within the bound.
A program may use at most 128 MiB of HBM per device.

```python
import math
import jax
import jax.numpy as jnp
from jax import lax

D = 256
PARENTS = 4
FINE_DEV = 16384
COARSE_DEV = 8192
DOMAINS = 64
FINE = 1048576
COARSE = 524288


def draw_parents(key, part):
    first_key, second_key, third_key = jax.random.split(jax.random.fold_in(key, 11), 3)
    blocks = jnp.broadcast_to((jnp.arange(FINE, dtype=jnp.int32) // FINE_DEV)[None, :], (PARENTS, FINE))
    offsets = jax.random.randint(first_key, (PARENTS, FINE), 0, COARSE_DEV)
    remote = jax.random.randint(second_key, (PARENTS, FINE), 0, 10) < 3
    sides = jax.random.randint(third_key, (PARENTS, FINE), 0, 2) * 2 - 1
    sides = jnp.where(blocks == 0, 1, jnp.where(blocks == DOMAINS - 1, -1, sides))
    window = 1 + jnp.where(remote, sides, 0)
    return (window * COARSE_DEV + offsets).astype(jnp.int32)


def draw_live_rows(key, part):
    first_key, second_key = jax.random.split(jax.random.fold_in(key, 23))
    counts = jax.random.randint(first_key, (DOMAINS,), FINE_DEV // 2, FINE_DEV + 1)
    full_block = jax.random.randint(second_key, (), 0, DOMAINS)
    return jnp.where(jnp.arange(DOMAINS) == full_block, FINE_DEV, counts).astype(jnp.int32)


def shard_levels(own_key, shape, cuts, smallest, top_value):
    gain, own = 1.0, jax.random.fold_in(own_key, 6)
    for dim, shards_of in cuts:
        draws = jnp.exp(jax.random.uniform(jax.random.fold_in(own, dim), (shards_of,), jnp.float32, smallest / len(cuts), top_value / len(cuts)))
        gain = gain * jnp.repeat(draws, shape[dim] // shards_of).reshape([-1 if axis == dim else 1 for axis in range(len(shape))])
    return gain


def scatter_about(key, dims, scale, bound, cuts=(), kind=jnp.bfloat16):
    values = scale * jax.random.normal(key, dims, jnp.float32)
    if cuts:
        values = values * shard_levels(key, dims, cuts, -0.22, 0.18)
    return jnp.clip(values, -bound, bound).astype(kind)


def setup_inputs(seed: int = 0) -> dict:
    streams_of = jax.random.split(jax.random.key(seed), 16)
    fine_latent = scatter_about(streams_of[0], (D, FINE), 1.0, 6.0, ((0, 8), (1, 64)))
    coarse_latent = scatter_about(streams_of[1], (D, COARSE), 1.0, 6.0, ((0, 8), (1, 64)))
    parents = draw_parents(jax.random.fold_in(streams_of[15], 71), 0)
    interp_weights = jnp.clip(jnp.exp(math.log(1.0) - 2.3025851 * jax.random.uniform(streams_of[3], (PARENTS, FINE), jnp.float32) ** shard_levels(streams_of[3], (PARENTS, FINE), ((1, 64),), -0.2, 0.2)), 0.1, 1.0)
    live_rows = draw_live_rows(jax.random.fold_in(streams_of[15], 71), 0)
    w_fine = scatter_about(streams_of[5], (D, D), (2 * D) ** -0.5, 0.25)
    w_parent = scatter_about(streams_of[6], (D, D), (2 * D) ** -0.5, 0.25)
    w_edge_out = scatter_about(streams_of[7], (D, D), D ** -0.5, 0.375)
    w_node_fine = scatter_about(streams_of[8], (D, D), (2 * D) ** -0.5, 0.25)
    w_node_agg = scatter_about(streams_of[9], (D, D), (2 * D) ** -0.5, 0.25)
    w_node_out = scatter_about(streams_of[10], (D, D), D ** -0.5, 0.375)
    edge_bias = scatter_about(streams_of[11], (D,), 0.5, 3.0, (), jnp.float32)
    node_bias = scatter_about(streams_of[12], (D,), 0.5, 3.0, (), jnp.float32)
    norm_gain = jnp.clip(1.0 + 0.18 * jax.random.normal(streams_of[13], (D,), jnp.float32), 0.1, 1.9)
    norm_bias = scatter_about(streams_of[14], (D,), 0.3, 2.0, (), jnp.float32)
    return {"fine_latent": fine_latent, "coarse_latent": coarse_latent, "parents": parents, "interp_weights": interp_weights, "live_rows": live_rows, "w_fine": w_fine, "w_parent": w_parent, "w_edge_out": w_edge_out, "w_node_fine": w_node_fine, "w_node_agg": w_node_agg, "w_node_out": w_node_out, "edge_bias": edge_bias, "node_bias": node_bias, "norm_gain": norm_gain, "norm_bias": norm_bias}


def update(latent, parent_rows, weights, params):
    w_fine, w_edge_out, w_node_fine, w_node_agg, w_node_out, edge_bias, node_bias, norm_gain, norm_bias = params
    fine_part = jnp.dot(latent, w_fine, preferred_element_type=jnp.float32) + edge_bias
    edge_hidden = jnp.maximum(fine_part[None] + parent_rows.astype(jnp.float32), 0.0).astype(jnp.bfloat16)
    width = edge_hidden.shape[2]
    message = jnp.dot(edge_hidden.reshape(-1, width), w_edge_out, preferred_element_type=jnp.float32).reshape(edge_hidden.shape)
    aggregate = lax.optimization_barrier(jnp.sum(weights[:, :, None] * message, axis=0)).astype(jnp.bfloat16)
    node_pre = jnp.dot(latent, w_node_fine, preferred_element_type=jnp.float32) + jnp.dot(aggregate, w_node_agg, preferred_element_type=jnp.float32) + node_bias
    node_hidden = jnp.maximum(node_pre, 0.0).astype(jnp.bfloat16)
    output = jnp.dot(node_hidden, w_node_out, preferred_element_type=jnp.float32)
    centre = lax.optimization_barrier(jnp.mean(output, axis=-1, keepdims=True))
    centered = output - centre
    spread = lax.optimization_barrier(jnp.mean(centered * centered, axis=-1, keepdims=True))
    normed = centered * lax.rsqrt(spread + 1e-05) * norm_gain + norm_bias
    return (latent.astype(jnp.float32) + normed).astype(jnp.bfloat16)

def reference(fine_latent, coarse_latent, parents, interp_weights, live_rows, w_fine, w_parent, w_edge_out, w_node_fine, w_node_agg, w_node_out, edge_bias, node_bias, norm_gain, norm_bias):
    params = (w_fine, w_edge_out, w_node_fine, w_node_agg, w_node_out, edge_bias, node_bias, norm_gain, norm_bias)
    projected = jnp.dot(coarse_latent.T, w_parent, preferred_element_type=jnp.float32).astype(jnp.bfloat16)
    latent_blocks = fine_latent.T.reshape(DOMAINS, FINE_DEV, D)
    parent_blocks = parents.reshape(PARENTS, DOMAINS, FINE_DEV).transpose(1, 0, 2)
    weight_blocks = interp_weights.reshape(PARENTS, DOMAINS, FINE_DEV).transpose(1, 0, 2)
    block_ids = jnp.arange(DOMAINS, dtype=jnp.int32)

    def one_block(packed):
        latent, parent_ids, weights, live_count, block = packed
        global_ids = (parent_ids + (block - 1) * COARSE_DEV).astype(jnp.int32)
        parent_rows = jnp.take(projected, global_ids, axis=0)
        updated = update(latent, parent_rows, weights, params)
        keep_rows = jnp.arange(FINE_DEV, dtype=jnp.int32) < live_count
        return jnp.where(keep_rows[:, None], updated, latent)
    result = lax.map(one_block, (latent_blocks, parent_blocks, weight_blocks, live_rows, block_ids))
    return result.reshape(FINE, D).T
```

```python
import jax
import jax.numpy as jnp
from jax import lax
from jax.experimental import pallas as pl
from jax.experimental.pallas import tpu as pltpu
from jax.sharding import PartitionSpec as P

MESH = pl.DeviceIdType.MESH
ANY = pl.BlockSpec(memory_space=pl.ANY)
VMEM = pl.BlockSpec(memory_space=pltpu.VMEM)
SMEM = pl.BlockSpec(memory_space=pltpu.SMEM)
DMA = pltpu.SemaphoreType.DMA
VMEM_LIMIT = 60 * 1024 * 1024

D = 256
HALF = 128
FEAT = 8
RING = 4
DOM = 64
SLICE = D // FEAT
PARTS = 4
PEERS = ((1, 0), (1, 1), (1, 3), (1, 2), (0, 1), (0, 3), (0, 2))
F32 = jnp.float32
BF16 = jnp.bfloat16


def dot(a, b, da, db):
    return lax.dot_general(a, b, (((da,), (db,)), ((), ())), preferred_element_type=F32)


def place():
    dom = lax.axis_index("dom")
    feat = lax.axis_index("feat")
    half = feat // RING
    ring = lax.rem(feat, RING)
    core = lax.rem(dom, 2)
    return dom, feat, half, ring, core


def feat_of(half, ring, a, b):
    return lax.rem(half + a, 2) * RING + lax.rem(ring + b, RING)


def seam_neighbour(dom, feat, core):
    target = lax.rem(dom + DOM + 2 * core - 1, DOM)
    low = lax.rem(dom // 2, 8)
    edge = jnp.where(core == 1, low == 7, low == 0)
    return target, jnp.where(edge, lax.rem(feat + RING, FEAT), feat)


def remote(src, dst, send, recv, device):
    return pltpu.make_async_remote_copy(
        src_ref=src, dst_ref=dst, send_sem=send, recv_sem=recv, device_id=device, device_id_type=MESH
    )


def collect_kernel(
    coarse, fine, w_parent, table, fine_full,
    landed, rows, c_s, c_r, f_s, f_r, n_s, n_r, p_s, p_r, z_s, z_r, local,
):
    dom, feat, half, ring, core = place()
    block = coarse.shape[1]
    share = block // RING
    part = share // PARTS
    mine = fine_full.shape[1]
    partner = (dom + 1 - 2 * core, feat)
    outer = seam_neighbour(dom, feat, core)
    up = (dom, feat_of(half, ring, 0, 1))
    down = (dom, feat_of(half, ring, 0, 3))
    own_base = block
    pair_base = core * 2 * block
    outer_base = (1 - core) * 2 * block
    edge_base = core * 2 * block

    barrier = pltpu.get_barrier_semaphore()
    friends = [(dom, feat_of(half, ring, a, b)) for a, b in PEERS] + [partner, outer]
    for friend in friends:
        pl.semaphore_signal(barrier, inc=1, device_id=friend, device_id_type=MESH)
    pl.semaphore_wait(barrier, len(friends))

    def aligned(x, m):
        return pl.multiple_of(x, m)

    def table_part(base, owner, q):
        return table.at[pl.ds(aligned(base + owner * share + q * part, part), part)]

    sends = []

    def go(copy):
        copy.start()
        sends.append(copy)

    my_rows = pl.ds(aligned(feat * SLICE, SLICE), SLICE)

    def coarse_out(q):
        for i, (a, b) in enumerate(PEERS):
            to = lax.rem(ring + b, RING)
            go(remote(
                coarse.at[:, pl.ds(aligned(to * share + q * part, part), part)],
                landed.at[my_rows, pl.ds(q * part, part)],
                c_s.at[i, q], c_r.at[i, q], (dom, feat_of(half, ring, a, b)),
            ))

    def coarse_in(q):
        for i in range(len(PEERS)):
            ref = landed.at[pl.ds(0, SLICE), pl.ds(q * part, part)]
            remote(ref, ref, c_s.at[i, q], c_r.at[i, q], partner).wait_recv()

    def fine_out(i):
        a, b = PEERS[i]
        to = feat_of(half, ring, a, b)
        go(remote(
            fine.at[:, pl.ds(aligned(to * mine, mine), mine)],
            fine_full.at[my_rows, :],
            f_s.at[i], f_r.at[i], (dom, to),
        ))

    def arrived(ref, recv, send):
        remote(ref, ref, send, recv, partner).wait_recv()

    def spread(kind, base, q):
        src = rows.at[pl.ds(q * part, part)] if kind == 0 else table_part(base, ring, q)
        go(remote(src, table_part(base, ring, q), n_s.at[kind, 0, q], n_r.at[kind, 0, q], up))
        go(remote(src, table_part(base, ring, q), n_s.at[kind, 1, q], n_r.at[kind, 1, q], down))

    def pass_on(kind, base, q):
        below = lax.rem(ring + 3, RING)
        above = lax.rem(ring + 1, RING)
        arrived(table_part(base, below, q), n_r.at[kind, 0, q], n_s.at[kind, 0, q])
        if q % 2 == 0:
            ref = table_part(base, below, q)
            go(remote(ref, ref, n_s.at[kind, 2, q], n_r.at[kind, 2, q], up))
        arrived(table_part(base, above, q), n_r.at[kind, 1, q], n_s.at[kind, 1, q])
        if q % 2 == 1:
            ref = table_part(base, above, q)
            go(remote(ref, ref, n_s.at[kind, 2, q], n_r.at[kind, 2, q], down))
        if kind == 0:
            to_pair(below, q, 1)
            to_pair(above, q, 2)

    def far_in(kind, base, q):
        far = lax.rem(ring + 2, RING)
        arrived(table_part(base, far, q), n_r.at[kind, 2, q], n_s.at[kind, 2, q])
        if kind == 0:
            to_pair(far, q, 3)

    def to_pair(owner, q, i):
        src = rows.at[pl.ds(q * part, part)] if i == 0 else table_part(own_base, owner, q)
        go(remote(src, table_part(pair_base, owner, q), p_s.at[i, q], p_r.at[i, q], partner))

    keep_coarse = pltpu.make_async_copy(
        coarse.at[:, pl.ds(aligned(ring * share, share), share)], landed.at[my_rows, :], local.at[0]
    )
    keep_coarse.start()
    coarse_out(0)
    coarse_out(1)
    keep_fine = pltpu.make_async_copy(
        fine.at[:, pl.ds(aligned(feat * mine, mine), mine)], fine_full.at[my_rows, :], local.at[1]
    )
    keep_fine.start()
    keep_coarse.wait()
    keeps = [keep_fine]

    def project(q):
        coarse_in(q)
        columns = pl.ds(q * part, part)
        product = dot(landed[:, columns], w_parent[...], 0, 0).astype(BF16)
        rows[columns, :, :] = product.reshape(part, 2, HALF)
        spread(0, own_base, q)
        to_pair(ring, q, 0)
        go(remote(
            rows.at[columns], table_part(outer_base, ring, q), z_s.at[q], z_r.at[q], outer
        ))
        keep = pltpu.make_async_copy(rows.at[columns], table_part(own_base, ring, q), local.at[2 + q])
        keep.start()
        keeps.append(keep)

    def relay(q):
        pass_on(0, own_base, q)
        arrived(table_part(edge_base, ring, q), z_r.at[q], z_s.at[q])
        spread(1, edge_base, q)

    def relay_edge(q):
        far_in(0, own_base, q)
        pass_on(1, edge_base, q)

    for q in range(PARTS + 2):
        if q < PARTS:
            project(q)
            if q + 2 < PARTS:
                coarse_out(q + 2)
            if q == PARTS - 2:
                for i in range(4):
                    fine_out(i)
            if q == PARTS - 1:
                for i in range(4, 7):
                    fine_out(i)
        if 1 <= q <= PARTS:
            relay(q - 1)
        if q >= 2:
            relay_edge(q - 2)
    other_base = (1 - core) * 2 * block
    for q in range(PARTS):
        far_in(1, edge_base, q)
        for i in range(4):
            ref = table_part(other_base, i, q)
            arrived(ref, p_r.at[i, q], p_s.at[i, q])
    for i in range(len(PEERS)):
        ref = fine_full.at[pl.ds(0, SLICE), :]
        arrived(ref, f_r.at[i], f_s.at[i])
    for keep in keeps:
        keep.wait()
    for copy in sends:
        copy.wait_send()


def collect(coarse, fine, w_parent):
    block = coarse.shape[1]
    share = block // RING
    mine = fine.shape[1] // FEAT
    return pl.pallas_call(
        collect_kernel,
        out_shape=(
            jax.ShapeDtypeStruct((3 * block, 2, HALF), BF16),
            jax.ShapeDtypeStruct((D, mine), BF16),
        ),
        in_specs=[ANY, ANY, VMEM],
        out_specs=(ANY, ANY),
        scratch_shapes=[
            pltpu.VMEM((D, share), BF16),
            pltpu.VMEM((share, 2, HALF), BF16),
            DMA((7, PARTS)), DMA((7, PARTS)),
            DMA((7,)), DMA((7,)),
            DMA((2, 3, PARTS)), DMA((2, 3, PARTS)),
            DMA((4, PARTS)), DMA((4, PARTS)),
            DMA((PARTS,)), DMA((PARTS,)),
            DMA((2 + PARTS,)),
        ],
        compiler_params=pltpu.CompilerParams(
            collective_id=0, has_side_effects=True, vmem_limit_bytes=VMEM_LIMIT
        ),
    )(coarse, fine, w_parent)


def column(ref):
    return jnp.transpose(jnp.broadcast_to(ref[...], (8, D)))[:, 0:1]


STEP = 512
UNROLL = 8


def nodes_kernel(
    parents, weights, live, table, fine, w_fine, w_edge_out, w_node_fine, w_node_agg, w_node_out,
    edge_bias, node_bias, norm_gain, norm_bias, out,
    near, pre, hidden, sem,
):
    load = pltpu.make_async_copy(table, near, sem)
    load.start()
    mine = fine.shape[1]
    first = lax.axis_index("feat") * mine
    node_col, gain_col, bias_col = column(node_bias), column(norm_gain), column(norm_bias)

    for step in range(mine // STEP):
        latent = fine[:, step * STEP:(step + 1) * STEP]
        fine_part = dot(latent, w_fine[...], 0, 0) + edge_bias[...]
        pre[...] = fine_part.reshape(STEP, 2, HALF)
        if step == 0:
            load.wait()

        def gather(j, carry):
            for u in range(UNROLL):
                i = j * UNROLL + u
                own = pre[i]
                total = None
                for k in range(PARENTS):
                    slot = parents[k, step * STEP + i]
                    value = jnp.maximum(own + near[slot].astype(F32), 0.0)
                    value = value.astype(BF16).astype(F32) * weights[k, step * STEP + i]
                    total = value if total is None else total + value
                hidden[i] = total
            return carry

        lax.fori_loop(0, STEP // UNROLL, gather, 0)
        mixed = hidden[...].reshape(STEP, D).astype(BF16)
        aggregate = dot(w_edge_out[...], mixed, 0, 1).astype(BF16)
        node_pre = dot(w_node_fine[...], latent, 0, 0) + dot(w_node_agg[...], aggregate, 0, 0) + node_col
        node_hidden = jnp.maximum(node_pre, 0.0).astype(BF16)
        update = dot(w_node_out[...], node_hidden, 0, 0)
        centre = jnp.mean(update, axis=0, keepdims=True)
        centered = update - centre
        spread = jnp.mean(centered * centered, axis=0, keepdims=True)
        normed = centered * lax.rsqrt(spread + 1e-05) * gain_col + bias_col
        updated = (latent.astype(F32) + normed).astype(BF16)
        position = first + step * STEP + lax.broadcasted_iota(jnp.int32, (1, STEP), 1)
        out[:, step * STEP:(step + 1) * STEP] = jnp.where(position < live[0], updated, latent)


PARENTS = 4


def nodes(parents, weights, live, table, fine, *params):
    mine = fine.shape[1]
    return pl.pallas_call(
        nodes_kernel,
        out_shape=jax.ShapeDtypeStruct((D, mine), BF16),
        in_specs=[SMEM, SMEM, SMEM, ANY] + [VMEM] * 10,
        out_specs=VMEM,
        scratch_shapes=[
            pltpu.VMEM(table.shape, BF16),
            pltpu.VMEM((STEP, 2, HALF), F32),
            pltpu.VMEM((STEP, 2, HALF), F32),
            DMA,
        ],
        compiler_params=pltpu.CompilerParams(vmem_limit_bytes=VMEM_LIMIT),
    )(parents, weights, live, table, fine, *params)


def deliver_kernel(result, out, send, recv, local):
    dom, feat, half, ring, core = place()
    mine = result.shape[1]
    barrier = pltpu.get_barrier_semaphore()
    for a, b in PEERS:
        pl.semaphore_signal(
            barrier, inc=1, device_id=(dom, feat_of(half, ring, a, b)), device_id_type=MESH
        )
    pl.semaphore_wait(barrier, len(PEERS))
    here = out.at[:, pl.ds(pl.multiple_of(feat * mine, mine), mine)]
    copies = []
    for i, (a, b) in enumerate(PEERS):
        to = feat_of(half, ring, a, b)
        copy = remote(
            result.at[pl.ds(pl.multiple_of(to * SLICE, SLICE), SLICE), :], here,
            send.at[i], recv.at[i], (dom, to),
        )
        copy.start()
        copies.append(copy)
    keep = pltpu.make_async_copy(
        result.at[pl.ds(pl.multiple_of(feat * SLICE, SLICE), SLICE), :], here, local
    )
    keep.start()
    keep.wait()
    for copy in copies:
        copy.wait()


def deliver(result, fine_count):
    return pl.pallas_call(
        deliver_kernel,
        out_shape=jax.ShapeDtypeStruct((SLICE, fine_count), BF16),
        in_specs=[ANY],
        out_specs=ANY,
        scratch_shapes=[DMA((7,)), DMA((7,)), DMA],
        compiler_params=pltpu.CompilerParams(collective_id=1, has_side_effects=True),
    )(result)


def shards(
    fine_latent, coarse_latent, parents, interp_weights, live_rows, w_fine, w_parent, w_edge_out,
    w_node_fine, w_node_agg, w_node_out, edge_bias, node_bias, norm_gain, norm_bias,
):
    mine = fine_latent.shape[1] // FEAT
    first = lax.axis_index("feat") * mine
    my_parents = lax.dynamic_slice_in_dim(parents, first, mine, 1)
    my_weights = lax.dynamic_slice_in_dim(interp_weights, first, mine, 1)
    table, fine = collect(coarse_latent, fine_latent, w_parent)
    result = nodes(
        my_parents, my_weights, live_rows, table, fine, w_fine, w_edge_out, w_node_fine,
        w_node_agg, w_node_out, edge_bias[None], node_bias[None], norm_gain[None], norm_bias[None],
    )
    return deliver(result, fine_latent.shape[1])


def solution(mesh):
    in_specs = (
        P("feat", "dom"), P("feat", "dom"), P(None, "dom"), P(None, "dom"), P("dom"),
        P(), P(), P(), P(), P(), P(), P(), P(), P(), P(),
    )
    return jax.shard_map(
        shards, mesh=mesh, in_specs=in_specs, out_specs=P("feat", "dom"), check_vma=False
    )
```

```python
import jax
import jax.numpy as jnp
from jax import lax
from jax.experimental import pallas as pl
from jax.experimental.pallas import tpu as pltpu
from jax.sharding import PartitionSpec as P

MESH = pl.DeviceIdType.MESH
ANY = pl.BlockSpec(memory_space=pl.ANY)
VMEM = pl.BlockSpec(memory_space=pltpu.VMEM)
SMEM = pl.BlockSpec(memory_space=pltpu.SMEM)
DMA = pltpu.SemaphoreType.DMA
VMEM_LIMIT = 60 * 1024 * 1024

D = 256
HALF = 128
FEAT = 8
RING = 4
DOM = 64
SLICE = D // FEAT
PARTS = 4
PARENTS = 4
STEP = 512
UNROLL = 8
PEERS = ((1, 0), (1, 1), (1, 3), (1, 2), (0, 1), (0, 3), (0, 2))
F32 = jnp.float32
BF16 = jnp.bfloat16


def dot(a, b, da, db):
    return lax.dot_general(a, b, (((da,), (db,)), ((), ())), preferred_element_type=F32)


def place():
    dom = lax.axis_index("dom")
    feat = lax.axis_index("feat")
    half = feat // RING
    ring = lax.rem(feat, RING)
    core = lax.rem(dom, 2)
    return dom, feat, half, ring, core


def feat_of(half, ring, a, b):
    return lax.rem(half + a, 2) * RING + lax.rem(ring + b, RING)


def seam_neighbour(dom, feat, core):
    target = lax.rem(dom + DOM + 2 * core - 1, DOM)
    low = lax.rem(dom // 2, 8)
    edge = jnp.where(core == 1, low == 7, low == 0)
    return target, jnp.where(edge, lax.rem(feat + RING, FEAT), feat)


def remote(src, dst, send, recv, device):
    return pltpu.make_async_remote_copy(
        src_ref=src, dst_ref=dst, send_sem=send, recv_sem=recv, device_id=device, device_id_type=MESH
    )


def column(ref):
    return jnp.transpose(jnp.broadcast_to(ref[...], (8, D)))[:, 0:1]


def kernel(
    coarse, fine, parents, weights, live, w_parent, w_fine, w_edge_out, w_node_fine, w_node_agg,
    w_node_out, edge_bias, node_bias, norm_gain, norm_bias, out,
    landed, near, latents, result, pre, hidden, slots, scales,
    c_s, c_r, f_s, f_r, n_s, n_r, p_s, p_r, z_s, z_r, o_s, o_r, local, kept,
):
    dom, feat, half, ring, core = place()
    block = coarse.shape[1]
    share = block // RING
    part = share // PARTS
    mine = latents.shape[1]
    steps = mine // STEP
    partner = (dom + 1 - 2 * core, feat)
    outer = seam_neighbour(dom, feat, core)
    up = (dom, feat_of(half, ring, 0, 1))
    down = (dom, feat_of(half, ring, 0, 3))
    own_base = block
    edge_base = core * 2 * block
    other_base = (1 - core) * 2 * block

    def aligned(start, size):
        return pl.ds(pl.multiple_of(start, size), size)

    my_rows = aligned(feat * SLICE, SLICE)
    table_loads = (
        pltpu.make_async_copy(parents.at[:, aligned(feat * mine, mine)], slots, local.at[0]),
        pltpu.make_async_copy(weights.at[:, aligned(feat * mine, mine)], scales, local.at[1]),
        pltpu.make_async_copy(coarse.at[:, aligned(ring * share, share)], landed.at[my_rows, :], local.at[2]),
        pltpu.make_async_copy(fine.at[:, aligned(feat * mine, mine)], latents.at[my_rows, :], local.at[3]),
    )
    for load in table_loads:
        load.start()

    barrier = pltpu.get_barrier_semaphore()
    friends = [(dom, feat_of(half, ring, a, b)) for a, b in PEERS] + [partner, outer]
    for friend in friends:
        pl.semaphore_signal(barrier, inc=1, device_id=friend, device_id_type=MESH)
    pl.semaphore_wait(barrier, len(friends))

    def rows_of(base, owner, q):
        return near.at[aligned(base + owner * share + q * part, part)]

    sends = []

    def go(copy):
        copy.start()
        sends.append(copy)

    def arrived(ref, recv, send):
        remote(ref, ref, send, recv, partner).wait_recv()

    def coarse_out(q):
        for i, (a, b) in enumerate(PEERS):
            to = lax.rem(ring + b, RING)
            go(remote(
                coarse.at[:, aligned(to * share + q * part, part)],
                landed.at[my_rows, pl.ds(q * part, part)],
                c_s.at[i, q], c_r.at[i, q], (dom, feat_of(half, ring, a, b)),
            ))

    def coarse_in(q):
        for i in range(len(PEERS)):
            arrived(landed.at[pl.ds(0, SLICE), pl.ds(q * part, part)], c_r.at[i, q], c_s.at[i, q])

    def fine_out(j):
        for i, (a, b) in enumerate(PEERS):
            to = feat_of(half, ring, a, b)
            go(remote(
                fine.at[:, aligned(to * mine + j * STEP, STEP)],
                latents.at[my_rows, pl.ds(j * STEP, STEP)],
                f_s.at[i, j], f_r.at[i, j], (dom, to),
            ))

    def spread(kind, base, q):
        ref = rows_of(base, ring, q)
        go(remote(ref, ref, n_s.at[kind, 0, q], n_r.at[kind, 0, q], up))
        go(remote(ref, ref, n_s.at[kind, 1, q], n_r.at[kind, 1, q], down))

    def to_pair(owner, q, i):
        go(remote(
            rows_of(own_base, owner, q), rows_of(edge_base, owner, q), p_s.at[i, q], p_r.at[i, q], partner
        ))

    def pass_on(kind, base, q):
        below = lax.rem(ring + 3, RING)
        above = lax.rem(ring + 1, RING)
        ref = rows_of(base, below, q)
        arrived(ref, n_r.at[kind, 0, q], n_s.at[kind, 0, q])
        if q % 2 == 0:
            go(remote(ref, ref, n_s.at[kind, 2, q], n_r.at[kind, 2, q], up))
        ref = rows_of(base, above, q)
        arrived(ref, n_r.at[kind, 1, q], n_s.at[kind, 1, q])
        if q % 2 == 1:
            go(remote(ref, ref, n_s.at[kind, 2, q], n_r.at[kind, 2, q], down))
        if kind == 0:
            to_pair(below, q, 1)
            to_pair(above, q, 2)

    def far_in(kind, base, q):
        far = lax.rem(ring + 2, RING)
        arrived(rows_of(base, far, q), n_r.at[kind, 2, q], n_s.at[kind, 2, q])
        if kind == 0:
            to_pair(far, q, 3)

    def project(q):
        coarse_in(q)
        product = dot(landed[:, q * part:(q + 1) * part], w_parent[...], 0, 0).astype(BF16)
        near[aligned(own_base + ring * share + q * part, part), :, :] = product.reshape(part, 2, HALF)
        spread(0, own_base, q)
        ref = rows_of(own_base, ring, q)
        go(remote(ref, rows_of(other_base, ring, q), z_s.at[q], z_r.at[q], outer))
        to_pair(ring, q, 0)

    def relay(q):
        pass_on(0, own_base, q)
        arrived(rows_of(edge_base, ring, q), z_r.at[q], z_s.at[q])
        spread(1, edge_base, q)

    def relay_edge(q):
        far_in(0, own_base, q)
        pass_on(1, edge_base, q)

    coarse_out(0)
    coarse_out(1)
    for load in table_loads:
        load.wait()
    for q in range(PARTS + 2):
        if q < PARTS:
            project(q)
            if q + 2 < PARTS:
                coarse_out(q + 2)
        if 2 <= q:
            for j in range((q - 2) * steps // PARTS, (q - 1) * steps // PARTS):
                fine_out(j)
        if 1 <= q <= PARTS:
            relay(q - 1)
        if 2 <= q:
            relay_edge(q - 2)
    for q in range(PARTS):
        far_in(1, edge_base, q)
        for i in range(4):
            arrived(rows_of(other_base, i, q), p_r.at[i, q], p_s.at[i, q])

    node_col, gain_col, bias_col = column(node_bias), column(norm_gain), column(norm_bias)
    here = feat * mine

    def deliver(j, i):
        a, b = PEERS[i]
        to = feat_of(half, ring, a, b)
        return remote(
            result.at[aligned(to * SLICE, SLICE), aligned(j * STEP, STEP)],
            out.at[:, aligned(here + j * STEP, STEP)],
            o_s.at[i, j], o_r.at[i, j], (dom, to),
        )

    def keep(j):
        return pltpu.make_async_copy(
            result.at[my_rows, aligned(j * STEP, STEP)], out.at[:, aligned(here + j * STEP, STEP)], kept.at[j]
        )

    def step(j, carry):
        columns = aligned(j * STEP, STEP)
        for i in range(len(PEERS)):
            arrived(latents.at[pl.ds(0, SLICE), columns], f_r.at[i, j], f_s.at[i, j])
        latent = latents[:, columns]
        fine_part = dot(latent, w_fine[...], 0, 0) + edge_bias[...]
        pre[...] = fine_part.reshape(STEP, 2, HALF)

        def gather(n, carry):
            for u in range(UNROLL):
                i = n * UNROLL + u
                own = pre[i]
                total = None
                for k in range(PARENTS):
                    value = jnp.maximum(own + near[slots[k, j * STEP + i]].astype(F32), 0.0)
                    value = value.astype(BF16).astype(F32) * scales[k, j * STEP + i]
                    total = value if total is None else total + value
                hidden[i] = total
            return carry

        lax.fori_loop(0, STEP // UNROLL, gather, 0)
        mixed = hidden[...].reshape(STEP, D).astype(BF16)
        aggregate = dot(w_edge_out[...], mixed, 0, 1).astype(BF16)
        node_pre = dot(w_node_fine[...], latent, 0, 0) + dot(w_node_agg[...], aggregate, 0, 0) + node_col
        node_hidden = jnp.maximum(node_pre, 0.0).astype(BF16)
        update = dot(w_node_out[...], node_hidden, 0, 0)
        centre = jnp.mean(update, axis=0, keepdims=True)
        centered = update - centre
        spread_out = jnp.mean(centered * centered, axis=0, keepdims=True)
        normed = centered * lax.rsqrt(spread_out + 1e-05) * gain_col + bias_col
        updated = (latent.astype(F32) + normed).astype(BF16)
        position = here + j * STEP + lax.broadcasted_iota(jnp.int32, (1, STEP), 1)
        result[:, columns] = jnp.where(position < live[0], updated, latent)
        for i in range(len(PEERS)):
            deliver(j, i).start()
        keep(j).start()
        return carry

    lax.fori_loop(0, steps, step, 0)
    for copy in sends:
        copy.wait_send()

    def finish(j, carry):
        keep(j).wait()
        for i in range(len(PEERS)):
            deliver(j, i).wait()
        return carry

    lax.fori_loop(0, steps, finish, 0)


def shards(
    fine_latent, coarse_latent, parents, interp_weights, live_rows, w_fine, w_parent, w_edge_out,
    w_node_fine, w_node_agg, w_node_out, edge_bias, node_bias, norm_gain, norm_bias,
):
    fine_count = fine_latent.shape[1]
    block = coarse_latent.shape[1]
    mine = fine_count // FEAT
    steps = mine // STEP
    return pl.pallas_call(
        kernel,
        out_shape=jax.ShapeDtypeStruct((SLICE, fine_count), BF16),
        in_specs=[ANY, ANY, ANY, ANY, SMEM] + [VMEM] * 10,
        out_specs=ANY,
        scratch_shapes=[
            pltpu.VMEM((D, block // RING), BF16),
            pltpu.VMEM((3 * block, 2, HALF), BF16),
            pltpu.VMEM((D, mine), BF16),
            pltpu.VMEM((D, mine), BF16),
            pltpu.VMEM((STEP, 2, HALF), F32),
            pltpu.VMEM((STEP, 2, HALF), F32),
            pltpu.SMEM((PARENTS, mine), jnp.int32),
            pltpu.SMEM((PARENTS, mine), F32),
            DMA((7, PARTS)), DMA((7, PARTS)),
            DMA((7, steps)), DMA((7, steps)),
            DMA((2, 3, PARTS)), DMA((2, 3, PARTS)),
            DMA((4, PARTS)), DMA((4, PARTS)),
            DMA((PARTS,)), DMA((PARTS,)),
            DMA((7, steps)), DMA((7, steps)),
            DMA((4,)), DMA((steps,)),
        ],
        compiler_params=pltpu.CompilerParams(
            collective_id=0, has_side_effects=True, vmem_limit_bytes=VMEM_LIMIT
        ),
    )(
        coarse_latent, fine_latent, parents, interp_weights, live_rows, w_parent, w_fine, w_edge_out,
        w_node_fine, w_node_agg, w_node_out, edge_bias[None], node_bias[None], norm_gain[None],
        norm_bias[None],
    )


def solution(mesh):
    in_specs = (
        P("feat", "dom"), P("feat", "dom"), P(None, "dom"), P(None, "dom"), P("dom"),
        P(), P(), P(), P(), P(), P(), P(), P(), P(), P(),
    )
    return jax.shard_map(
        shards, mesh=mesh, in_specs=in_specs, out_specs=P("feat", "dom"), check_vma=False
    )
```

```python
import jax
import jax.numpy as jnp
from jax import lax
from jax.experimental import pallas as pl
from jax.experimental.pallas import tpu as pltpu
from jax.sharding import PartitionSpec as P

MESH = pl.DeviceIdType.MESH
ANY = pl.BlockSpec(memory_space=pl.ANY)
VMEM = pl.BlockSpec(memory_space=pltpu.VMEM)
DMA = pltpu.SemaphoreType.DMA
VMEM_LIMIT = 60 * 1024 * 1024

D = 256
HALF = 128
FEAT = 8
RING = 4
SLICE = D // FEAT
PARTS = 4
PARENTS = 4
OWNERS = 8
STEP = 512
UNROLL = 8
F32 = jnp.float32
BF16 = jnp.bfloat16


def dot(a, b, da, db):
    return lax.dot_general(a, b, (((da,), (db,)), ((), ())), preferred_element_type=F32)


def remote(src, dst, send, recv, device):
    return pltpu.make_async_remote_copy(
        src_ref=src, dst_ref=dst, send_sem=send, recv_sem=recv, device_id=device, device_id_type=MESH
    )


def column(ref):
    return jnp.transpose(jnp.broadcast_to(ref[...], (8, D)))[:, 0:1]


def device(x, y, z, core):
    return x * 16 + lax.rem(z, 8) * 2 + core, (z // 8) * RING + y


def kernel(
    coarse, fine, parents, weights, w_parent, w_fine, w_edge_out, w_node_fine, w_node_agg,
    w_node_out, edge_bias, node_bias, norm_gain, norm_bias, out, slots_in, scales_in,
    coarse_held, fine_held, landed, near, latents, result, back, pre, hidden,
    slots, scales,
    hc_s, hc_r, hf_s, hf_r, c_s, c_r, f_s, f_r, n_s, n_r, p_s, p_r, e_s, e_r,
    a_s, a_r, b_s, b_r, o_s, o_r, w_s, w_r, local,
):
    dom = lax.axis_index("dom")
    feat = lax.axis_index("feat")
    x, j_own, core = dom // 16, lax.rem(dom // 2, 8), lax.rem(dom, 2)
    half, y = feat // RING, lax.rem(feat, RING)
    z = half * 8 + j_own
    kind_x = lax.rem(x, 2)
    base_x = x - kind_x
    owner = y * 2 + core
    swapped = kind_x != core
    block = coarse.shape[1]
    part = block // OWNERS // PARTS
    group = OWNERS * part
    mine = latents.shape[1]
    steps = mine // STEP
    wide = OWNERS * STEP

    def aligned(start, size):
        return pl.ds(pl.multiple_of(start, size), size)

    work_z = lax.rem(j_own + 8 * core + 4, 16)
    from_u = lax.rem(z + 12, 16)
    from_j, from_core = lax.rem(from_u, 8), from_u // 8

    def worker(y_to, core_to):
        return device(x, y_to, work_z, core_to)

    def holder(y_to, half_to):
        return device(x, y_to, from_j + 8 * half_to, from_core)

    twin = device(base_x + 1 - kind_x, y, z, 1 - core)
    partner = device(x, y, z, 1 - core)
    up = device(x, lax.rem(y + 1, RING), z, core)
    down = device(x, lax.rem(y + 3, RING), z, core)
    flat = device(base_x + 1 - kind_x, y, z, core)
    turn = jnp.where(kind_x == 0, z == 4, z == 3)
    inside = base_x + 1 - kind_x
    across = lax.rem(x + 3 + 2 * kind_x, 4)
    slant = device(
        jnp.where(turn, across, inside), y, lax.rem(z + 15 + 2 * kind_x, 16), core
    )
    edges_to = device(base_x + core, y, lax.rem(j_own + 8 * kind_x + 4, 16), half)
    edges_from = device(base_x + from_core, y, from_j + 8 * core, kind_x)

    barrier = pltpu.get_barrier_semaphore()
    friends = [worker(lax.rem(y + b, RING), e) for b in range(RING) for e in range(2)]
    friends += [holder(lax.rem(y + b, RING), e) for b in range(RING) for e in range(2)]
    friends += [twin, partner, up, down, flat, slant, edges_to, edges_from]
    for friend in friends:
        pl.semaphore_signal(barrier, inc=1, device_id=friend, device_id_type=MESH)
    pl.semaphore_wait(barrier, len(friends))

    center_base = block
    flat_base = (1 - kind_x) * 2 * block
    slant_base = kind_x * 2 * block
    bases = (center_base, flat_base, slant_base)

    sends = []

    def go(copy):
        copy.start()
        sends.append(copy)

    def arrived(ref, recv, send):
        remote(ref, ref, send, recv, partner).wait_recv()

    def rows_of(base, who, q):
        return near.at[aligned(base + q * group + who * part, part)]

    def hold(src, dst, send, recv, kept, starting):
        there = remote(src, dst, send, recv, twin)
        here = pltpu.make_async_copy(src, dst, kept)

        @pl.when(swapped)
        def _():
            if starting:
                there.start()
            else:
                there.wait()

        @pl.when(jnp.logical_not(swapped))
        def _():
            if starting:
                here.start()
            else:
                here.wait()

    def hold_coarse(q, starting):
        columns = pl.ds(q * group, group)
        hold(coarse.at[:, columns], coarse_held.at[:, columns], hc_s.at[q], hc_r.at[q], local.at[q], starting)

    def hold_fine(j, starting):
        columns = pl.ds(j * wide, wide)
        hold(fine.at[:, columns], fine_held.at[:, columns], hf_s.at[j], hf_r.at[j], local.at[PARTS + j], starting)

    my_rows = aligned(feat * SLICE, SLICE)

    def coarse_out(q):
        hold_coarse(q, False)
        for b in range(RING):
            for e in range(2):
                to = lax.rem(y + b, RING)
                go(remote(
                    coarse_held.at[:, aligned(q * group + (to * 2 + e) * part, part)],
                    landed.at[my_rows, pl.ds(q * part, part)],
                    c_s.at[b * 2 + e, q], c_r.at[feat, q], worker(to, e),
                ))

    def fine_out(j):
        hold_fine(j, False)
        for b in range(RING):
            for e in range(2):
                to = lax.rem(y + b, RING)
                go(remote(
                    fine_held.at[:, aligned(j * wide + (to * 2 + e) * STEP, STEP)],
                    latents.at[my_rows, pl.ds(j * STEP, STEP)],
                    f_s.at[b * 2 + e, j], f_r.at[feat, j], worker(to, e),
                ))

    def edges_out():
        for j in range(steps):
            columns = aligned(j * wide + (y * 2 + half) * STEP, STEP)
            place = pl.ds(j * STEP, STEP)
            go(remote(parents.at[:, columns], slots_in.at[:, place], a_s.at[j], a_r.at[j], edges_to))
            go(remote(weights.at[:, columns], scales_in.at[:, place], b_s.at[j], b_r.at[j], edges_to))

    def edges_in():
        for j in range(steps):
            place = pl.ds(j * STEP, STEP)
            arrived(slots_in.at[:, place], a_r.at[j], a_s.at[j])
            arrived(scales_in.at[:, place], b_r.at[j], b_s.at[j])
        moves = (
            pltpu.make_async_copy(slots_in, slots, local.at[PARTS + steps]),
            pltpu.make_async_copy(scales_in, scales, local.at[PARTS + steps + 1]),
        )
        for move in moves:
            move.start()
        for move in moves:
            move.wait()

    def to_pair(kind, ring, i, q):
        ref = rows_of(bases[kind], ring * 2 + core, q)
        go(remote(ref, ref, p_s.at[kind, i, q], p_r.at[kind, i, q], partner))

    def spread(kind, q):
        ref = rows_of(bases[kind], owner, q)
        go(remote(ref, ref, n_s.at[kind, 0, q], n_r.at[kind, 0, q], up))
        go(remote(ref, ref, n_s.at[kind, 1, q], n_r.at[kind, 1, q], down))
        to_pair(kind, y, 0, q)

    def pass_on(kind, q):
        below, above = lax.rem(y + 3, RING), lax.rem(y + 1, RING)
        ref = rows_of(bases[kind], below * 2 + core, q)
        arrived(ref, n_r.at[kind, 0, q], n_s.at[kind, 0, q])
        if q % 2 == 0:
            go(remote(ref, ref, n_s.at[kind, 2, q], n_r.at[kind, 2, q], up))
        ref = rows_of(bases[kind], above * 2 + core, q)
        arrived(ref, n_r.at[kind, 1, q], n_s.at[kind, 1, q])
        if q % 2 == 1:
            go(remote(ref, ref, n_s.at[kind, 2, q], n_r.at[kind, 2, q], down))
        to_pair(kind, below, 1, q)
        to_pair(kind, above, 2, q)

    def far_in(kind, q):
        far = lax.rem(y + 2, RING)
        arrived(rows_of(bases[kind], far * 2 + core, q), n_r.at[kind, 2, q], n_s.at[kind, 2, q])
        to_pair(kind, far, 3, q)

    def project(q):
        for s in range(OWNERS):
            arrived(landed.at[pl.ds(0, SLICE), pl.ds(q * part, part)], c_r.at[s, q], c_s.at[s, q])
        product = dot(landed[:, q * part:(q + 1) * part], w_parent[...], 0, 0).astype(BF16)
        near[aligned(center_base + q * group + owner * part, part), :, :] = product.reshape(part, 2, HALF)
        ref = rows_of(center_base, owner, q)
        go(remote(ref, rows_of(slant_there, owner, q), e_s.at[1, q], e_r.at[1, q], slant))
        go(remote(ref, rows_of(flat_there, owner, q), e_s.at[0, q], e_r.at[0, q], flat))
        spread(0, q)

    flat_there = kind_x * 2 * block
    slant_there = (1 - kind_x) * 2 * block

    def relay(q):
        pass_on(0, q)
        for kind in (1, 2):
            arrived(rows_of(bases[kind], owner, q), e_r.at[kind - 1, q], e_s.at[kind - 1, q])
            spread(kind, q)

    def relay_edge(q):
        far_in(0, q)
        pass_on(1, q)
        pass_on(2, q)

    for q in range(PARTS):
        hold_coarse(q, True)
    hold_fine(0, True)
    coarse_out(0)
    coarse_out(1)
    for q in range(PARTS + 2):
        if q < PARTS:
            project(q)
            if q + 2 < PARTS:
                coarse_out(q + 2)
        if q + 1 < steps:
            hold_fine(q + 1, True)
        if q == 1:
            edges_out()
        if 2 <= q < 2 + steps:
            fine_out(q - 2)
        if 1 <= q <= PARTS:
            relay(q - 1)
        if 2 <= q:
            relay_edge(q - 2)
    for kind in (1, 2):
        for q in range(PARTS):
            far_in(kind, q)
    edges_in()
    for kind in range(3):
        for q in range(PARTS):
            for i in range(4):
                arrived(rows_of(bases[kind], i * 2 + 1 - core, q), p_r.at[kind, i, q], p_s.at[kind, i, q])

    node_col, gain_col, bias_col = column(node_bias), column(norm_gain), column(norm_bias)

    def deliver(j, b, e):
        to = lax.rem(y + b, RING)
        return remote(
            result.at[aligned((e * RING + to) * SLICE, SLICE), aligned(j * STEP, STEP)],
            back.at[:, aligned(j * wide + owner * STEP, STEP)],
            o_s.at[b * 2 + e, j], o_r.at[owner, j], holder(to, e),
        )

    def hand_back(j, starting):
        columns = aligned(j * wide, wide)
        hold(back.at[:, columns], out.at[:, columns], w_s.at[j], w_r.at[j], local.at[j], starting)

    def returned(j):
        for s in range(OWNERS):
            arrived(back.at[:, aligned(j * wide, STEP)], o_r.at[s, j], o_s.at[s, j])
        hand_back(j, True)

    def step(j, carry):
        columns = aligned(j * STEP, STEP)
        for s in range(OWNERS):
            arrived(latents.at[pl.ds(0, SLICE), columns], f_r.at[s, j], f_s.at[s, j])
        latent = latents[:, columns]
        fine_part = dot(latent, w_fine[...], 0, 0) + edge_bias[...]
        pre[...] = fine_part.reshape(STEP, 2, HALF)

        def gather(n, carry):
            for u in range(UNROLL):
                i = n * UNROLL + u
                own = pre[i]
                total = None
                for k in range(PARENTS):
                    value = jnp.maximum(own + near[slots[k, j * STEP + i]].astype(F32), 0.0)
                    value = value.astype(BF16).astype(F32) * scales[k, j * STEP + i]
                    total = value if total is None else total + value
                hidden[i] = total
            return carry

        lax.fori_loop(0, STEP // UNROLL, gather, 0)
        mixed = hidden[...].reshape(STEP, D).astype(BF16)
        aggregate = dot(w_edge_out[...], mixed, 0, 1).astype(BF16)
        node_pre = dot(w_node_fine[...], latent, 0, 0) + dot(w_node_agg[...], aggregate, 0, 0) + node_col
        node_hidden = jnp.maximum(node_pre, 0.0).astype(BF16)
        update = dot(w_node_out[...], node_hidden, 0, 0)
        centre = jnp.mean(update, axis=0, keepdims=True)
        centered = update - centre
        variance = jnp.mean(centered * centered, axis=0, keepdims=True)
        normed = centered * lax.rsqrt(variance + 1e-05) * gain_col + bias_col
        result[:, columns] = (latent.astype(F32) + normed).astype(BF16)
        for b in range(RING):
            for e in range(2):
                deliver(j, b, e).start()

        @pl.when(j > 0)
        def _():
            returned(j - 1)

        return carry

    lax.fori_loop(0, steps, step, 0)
    returned(steps - 1)
    for copy in sends:
        copy.wait_send()

    def finish(j, carry):
        hand_back(j, False)
        for b in range(RING):
            for e in range(2):
                deliver(j, b, e).wait_send()
        return carry

    lax.fori_loop(0, steps, finish, 0)


def shards(
    fine_latent, coarse_latent, parents, interp_weights, live_rows, w_fine, w_parent, w_edge_out,
    w_node_fine, w_node_agg, w_node_out, edge_bias, node_bias, norm_gain, norm_bias,
):
    fine_count = fine_latent.shape[1]
    block = coarse_latent.shape[1]
    mine = fine_count // OWNERS
    steps = mine // STEP
    pairs = [
        (PARTS,), (steps,), (OWNERS, PARTS), (OWNERS, steps), (3, 3, PARTS), (3, 4, PARTS),
        (2, PARTS), (steps,), (steps,), (OWNERS, steps), (steps,),
    ]
    updated, _, _ = pl.pallas_call(
        kernel,
        out_shape=(
            jax.ShapeDtypeStruct((SLICE, fine_count), BF16),
            jax.ShapeDtypeStruct((PARENTS, mine), jnp.int32),
            jax.ShapeDtypeStruct((PARENTS, mine), F32),
        ),
        in_specs=[ANY] * 4 + [VMEM] * 10,
        out_specs=(ANY, ANY, ANY),
        scratch_shapes=[
            pltpu.VMEM((SLICE, block), BF16),
            pltpu.VMEM((SLICE, fine_count), BF16),
            pltpu.VMEM((D, block // OWNERS), BF16),
            pltpu.VMEM((3 * block, 2, HALF), BF16),
            pltpu.VMEM((D, mine), BF16),
            pltpu.VMEM((D, mine), BF16),
            pltpu.VMEM((SLICE, fine_count), BF16),
            pltpu.VMEM((STEP, 2, HALF), F32),
            pltpu.VMEM((STEP, 2, HALF), F32),
            pltpu.SMEM((PARENTS, mine), jnp.int32),
            pltpu.SMEM((PARENTS, mine), F32),
        ] + [DMA(shape) for shape in pairs for _ in range(2)] + [DMA((PARTS + steps + 2,))],
        compiler_params=pltpu.CompilerParams(
            collective_id=0, has_side_effects=True, vmem_limit_bytes=VMEM_LIMIT
        ),
    )(
        coarse_latent, fine_latent, parents, interp_weights, w_parent, w_fine, w_edge_out,
        w_node_fine, w_node_agg, w_node_out, edge_bias[None], node_bias[None], norm_gain[None],
        norm_bias[None],
    )
    live = jnp.arange(fine_count, dtype=jnp.int32) < live_rows[0]
    return jnp.where(live[None, :], updated, fine_latent)


def solution(mesh):
    in_specs = (
        P("feat", "dom"), P("feat", "dom"), P(None, "dom"), P(None, "dom"), P("dom"),
        P(), P(), P(), P(), P(), P(), P(), P(), P(), P(),
    )
    return jax.shard_map(
        shards, mesh=mesh, in_specs=in_specs, out_specs=P("feat", "dom"), check_vma=False
    )
```

```python
import jax
import jax.numpy as jnp
from jax import lax
from jax.experimental import pallas as pl
from jax.experimental.pallas import tpu as pltpu
from jax.sharding import PartitionSpec as P

MESH = pl.DeviceIdType.MESH
ANY = pl.BlockSpec(memory_space=pl.ANY)
VMEM = pl.BlockSpec(memory_space=pltpu.VMEM)
DMA = pltpu.SemaphoreType.DMA
VMEM_LIMIT = 60 * 1024 * 1024

D = 256
HALF = 128
FEAT = 8
RING = 4
SLICE = D // FEAT
PARTS = 4
PARENTS = 4
OWNERS = 8
STEP = 512
UNROLL = 8
F32 = jnp.float32
BF16 = jnp.bfloat16


def dot(a, b, da, db):
    return lax.dot_general(a, b, (((da,), (db,)), ((), ())), preferred_element_type=F32)


def remote(src, dst, send, recv, device):
    return pltpu.make_async_remote_copy(
        src_ref=src, dst_ref=dst, send_sem=send, recv_sem=recv, device_id=device, device_id_type=MESH
    )


def column(ref):
    return jnp.transpose(jnp.broadcast_to(ref[...], (8, D)))[:, 0:1]


def device(x, y, z, core):
    return x * 16 + lax.rem(z, 8) * 2 + core, (z // 8) * RING + y


def kernel(
    coarse, fine, parents, weights, w_parent, w_fine, w_edge_out, w_node_fine, w_node_agg,
    w_node_out, edge_bias, node_bias, norm_gain, norm_bias, out, slots_in, scales_in,
    coarse_held, fine_held, landed, near, latents, result, back, pre, hidden,
    slots, scales,
    hc_s, hc_r, hf_s, hf_r, c_s, c_r, f_s, f_r, n_s, n_r, p_s, p_r, e_s, e_r,
    a_s, a_r, b_s, b_r, o_s, o_r, w_s, w_r, local,
):
    dom = lax.axis_index("dom")
    feat = lax.axis_index("feat")
    x, j_own, core = dom // 16, lax.rem(dom // 2, 8), lax.rem(dom, 2)
    half, y = feat // RING, lax.rem(feat, RING)
    z = half * 8 + j_own
    kind_x = lax.rem(x, 2)
    base_x = x - kind_x
    owner = y * 2 + core
    swapped = kind_x != core
    block = coarse.shape[1]
    part = block // OWNERS // PARTS
    group = OWNERS * part
    mine = latents.shape[1]
    steps = mine // STEP
    wide = OWNERS * STEP

    def aligned(start, size):
        return pl.ds(pl.multiple_of(start, size), size)

    work_z = lax.rem(j_own + 8 * core + 4, 16)
    from_u = lax.rem(z + 12, 16)
    from_j, from_core = lax.rem(from_u, 8), from_u // 8

    def worker(y_to, core_to):
        return device(x, y_to, work_z, core_to)

    def holder(y_to, half_to):
        return device(x, y_to, from_j + 8 * half_to, from_core)

    twin = device(base_x + 1 - kind_x, y, z, 1 - core)
    partner = device(x, y, z, 1 - core)
    up = device(x, lax.rem(y + 1, RING), z, core)
    down = device(x, lax.rem(y + 3, RING), z, core)
    flat = device(base_x + 1 - kind_x, y, z, core)
    turn = jnp.where(kind_x == 0, z == 4, z == 3)
    inside = base_x + 1 - kind_x
    across = lax.rem(x + 3 + 2 * kind_x, 4)
    slant = device(
        jnp.where(turn, across, inside), y, lax.rem(z + 15 + 2 * kind_x, 16), core
    )
    edges_to = device(base_x + core, y, lax.rem(j_own + 8 * kind_x + 4, 16), half)
    edges_from = device(base_x + from_core, y, from_j + 8 * core, kind_x)

    barrier = pltpu.get_barrier_semaphore()
    friends = [worker(lax.rem(y + b, RING), e) for b in range(RING) for e in range(2)]
    friends += [holder(lax.rem(y + b, RING), e) for b in range(RING) for e in range(2)]
    friends += [twin, partner, up, down, flat, slant, edges_to, edges_from]
    for friend in friends:
        pl.semaphore_signal(barrier, inc=1, device_id=friend, device_id_type=MESH)
    pl.semaphore_wait(barrier, len(friends))

    center_base = block
    flat_base = (1 - kind_x) * 2 * block
    slant_base = kind_x * 2 * block
    bases = (center_base, flat_base, slant_base)

    sends = []

    def go(copy):
        copy.start()
        sends.append(copy)

    def arrived(ref, recv, send):
        remote(ref, ref, send, recv, partner).wait_recv()

    def rows_of(base, who, q):
        return near.at[aligned(base + q * group + who * part, part)]

    def hold(src, dst, send, recv, kept, starting):
        there = remote(src, dst, send, recv, twin)
        here = pltpu.make_async_copy(src, dst, kept)

        @pl.when(swapped)
        def _():
            if starting:
                there.start()
            else:
                there.wait()

        @pl.when(jnp.logical_not(swapped))
        def _():
            if starting:
                here.start()
            else:
                here.wait()

    def hold_coarse(q, starting):
        columns = pl.ds(q * group, group)
        hold(coarse.at[:, columns], coarse_held.at[:, columns], hc_s.at[q], hc_r.at[q], local.at[q], starting)

    def hold_fine(j, starting):
        columns = pl.ds(j * wide, wide)
        hold(fine.at[:, columns], fine_held.at[:, columns], hf_s.at[j], hf_r.at[j], local.at[PARTS + j], starting)

    my_rows = aligned(feat * SLICE, SLICE)

    def coarse_out(q):
        hold_coarse(q, False)
        for b in range(RING):
            for e in range(2):
                to = lax.rem(y + b, RING)
                go(remote(
                    coarse_held.at[:, aligned(q * group + (to * 2 + e) * part, part)],
                    landed.at[my_rows, pl.ds(q * part, part)],
                    c_s.at[b * 2 + e, q], c_r.at[feat, q], worker(to, e),
                ))

    def fine_out(j):
        hold_fine(j, False)
        for b in range(RING):
            for e in range(2):
                to = lax.rem(y + b, RING)
                go(remote(
                    fine_held.at[:, aligned(j * wide + (to * 2 + e) * STEP, STEP)],
                    latents.at[my_rows, pl.ds(j * STEP, STEP)],
                    f_s.at[b * 2 + e, j], f_r.at[feat, j], worker(to, e),
                ))

    def edges_out():
        for j in range(steps):
            columns = aligned(j * wide + (y * 2 + half) * STEP, STEP)
            place = pl.ds(j * STEP, STEP)
            go(remote(parents.at[:, columns], slots_in.at[:, place], a_s.at[j], a_r.at[j], edges_to))
            go(remote(weights.at[:, columns], scales_in.at[:, place], b_s.at[j], b_r.at[j], edges_to))

    def edges_in():
        for j in range(steps):
            place = pl.ds(j * STEP, STEP)
            arrived(slots_in.at[:, place], a_r.at[j], a_s.at[j])
            arrived(scales_in.at[:, place], b_r.at[j], b_s.at[j])
        moves = (
            pltpu.make_async_copy(slots_in, slots, local.at[PARTS + steps]),
            pltpu.make_async_copy(scales_in, scales, local.at[PARTS + steps + 1]),
        )
        for move in moves:
            move.start()
        for move in moves:
            move.wait()

    def to_pair(kind, ring, i, q):
        ref = rows_of(bases[kind], ring * 2 + core, q)
        go(remote(ref, ref, p_s.at[kind, i, q], p_r.at[kind, i, q], partner))

    def spread(kind, q):
        ref = rows_of(bases[kind], owner, q)
        go(remote(ref, ref, n_s.at[kind, 0, q], n_r.at[kind, 0, q], up))
        go(remote(ref, ref, n_s.at[kind, 1, q], n_r.at[kind, 1, q], down))
        to_pair(kind, y, 0, q)

    def pass_on(kind, q):
        below, above = lax.rem(y + 3, RING), lax.rem(y + 1, RING)
        ref = rows_of(bases[kind], below * 2 + core, q)
        arrived(ref, n_r.at[kind, 0, q], n_s.at[kind, 0, q])
        if q % 2 == 0:
            go(remote(ref, ref, n_s.at[kind, 2, q], n_r.at[kind, 2, q], up))
        ref = rows_of(bases[kind], above * 2 + core, q)
        arrived(ref, n_r.at[kind, 1, q], n_s.at[kind, 1, q])
        if q % 2 == 1:
            go(remote(ref, ref, n_s.at[kind, 2, q], n_r.at[kind, 2, q], down))
        to_pair(kind, below, 1, q)
        to_pair(kind, above, 2, q)

    def far_in(kind, q):
        far = lax.rem(y + 2, RING)
        arrived(rows_of(bases[kind], far * 2 + core, q), n_r.at[kind, 2, q], n_s.at[kind, 2, q])
        to_pair(kind, far, 3, q)

    def project(q):
        for s in range(OWNERS):
            arrived(landed.at[pl.ds(0, SLICE), pl.ds(q * part, part)], c_r.at[s, q], c_s.at[s, q])
        product = dot(landed[:, q * part:(q + 1) * part], w_parent[...], 0, 0).astype(BF16)
        near[aligned(center_base + q * group + owner * part, part), :, :] = product.reshape(part, 2, HALF)
        ref = rows_of(center_base, owner, q)
        go(remote(ref, rows_of(slant_there, owner, q), e_s.at[1, q], e_r.at[1, q], slant))
        go(remote(ref, rows_of(flat_there, owner, q), e_s.at[0, q], e_r.at[0, q], flat))
        spread(0, q)

    flat_there = kind_x * 2 * block
    slant_there = (1 - kind_x) * 2 * block

    def relay(q):
        pass_on(0, q)
        for kind in (1, 2):
            arrived(rows_of(bases[kind], owner, q), e_r.at[kind - 1, q], e_s.at[kind - 1, q])
            spread(kind, q)

    def relay_edge(q):
        far_in(0, q)
        pass_on(1, q)
        pass_on(2, q)

    for q in range(PARTS):
        hold_coarse(q, True)
    for j in range(steps // PARTS):
        hold_fine(j, True)
    coarse_out(0)
    coarse_out(1)
    for q in range(PARTS + 2):
        if q < PARTS:
            project(q)
            if q + 2 < PARTS:
                coarse_out(q + 2)
        if q + 1 < PARTS:
            for j in range((q + 1) * steps // PARTS, (q + 2) * steps // PARTS):
                hold_fine(j, True)
        if q == 1:
            edges_out()
        if 1 <= q <= PARTS:
            relay(q - 1)
        if 2 <= q:
            relay_edge(q - 2)
        if 2 <= q:
            for j in range((q - 2) * steps // PARTS, (q - 1) * steps // PARTS):
                fine_out(j)
    for kind in (1, 2):
        for q in range(PARTS):
            far_in(kind, q)
    edges_in()
    for kind in range(3):
        for q in range(PARTS):
            for i in range(4):
                arrived(rows_of(bases[kind], i * 2 + 1 - core, q), p_r.at[kind, i, q], p_s.at[kind, i, q])

    node_col, gain_col, bias_col = column(node_bias), column(norm_gain), column(norm_bias)

    def deliver(j, b, e):
        to = lax.rem(y + b, RING)
        return remote(
            result.at[aligned((e * RING + to) * SLICE, SLICE), aligned(j * STEP, STEP)],
            back.at[:, aligned(j * wide + owner * STEP, STEP)],
            o_s.at[b * 2 + e, j], o_r.at[owner, j], holder(to, e),
        )

    def hand_back(j, starting):
        columns = aligned(j * wide, wide)
        hold(back.at[:, columns], out.at[:, columns], w_s.at[j], w_r.at[j], local.at[PARTS + j], starting)

    def returned(j):
        for s in range(OWNERS):
            arrived(back.at[:, aligned(j * wide, STEP)], o_r.at[s, j], o_s.at[s, j])
        hand_back(j, True)

    def step(j, carry):
        columns = aligned(j * STEP, STEP)
        for s in range(OWNERS):
            arrived(latents.at[pl.ds(0, SLICE), columns], f_r.at[s, j], f_s.at[s, j])
        latent = latents[:, columns]
        fine_part = dot(latent, w_fine[...], 0, 0) + edge_bias[...]
        pre[...] = fine_part.reshape(STEP, 2, HALF)

        def gather(n, carry):
            for u in range(UNROLL):
                i = n * UNROLL + u
                own = pre[i]
                total = None
                for k in range(PARENTS):
                    value = jnp.maximum(own + near[slots[k, j * STEP + i]].astype(F32), 0.0)
                    value = value.astype(BF16).astype(F32) * scales[k, j * STEP + i]
                    total = value if total is None else total + value
                hidden[i] = total
            return carry

        lax.fori_loop(0, STEP // UNROLL, gather, 0)
        mixed = hidden[...].reshape(STEP, D).astype(BF16)
        aggregate = dot(w_edge_out[...], mixed, 0, 1).astype(BF16)
        node_pre = dot(w_node_fine[...], latent, 0, 0) + dot(w_node_agg[...], aggregate, 0, 0) + node_col
        node_hidden = jnp.maximum(node_pre, 0.0).astype(BF16)
        update = dot(w_node_out[...], node_hidden, 0, 0)
        centre = jnp.mean(update, axis=0, keepdims=True)
        centered = update - centre
        variance = jnp.mean(centered * centered, axis=0, keepdims=True)
        normed = centered * lax.rsqrt(variance + 1e-05) * gain_col + bias_col
        result[:, columns] = (latent.astype(F32) + normed).astype(BF16)
        for b in range(RING):
            for e in range(2):
                deliver(j, b, e).start()

        @pl.when(j > 0)
        def _():
            returned(j - 1)

        return carry

    lax.fori_loop(0, steps, step, 0)
    returned(steps - 1)
    for copy in sends:
        copy.wait_send()

    def finish(j, carry):
        hand_back(j, False)
        for b in range(RING):
            for e in range(2):
                deliver(j, b, e).wait_send()
        return carry

    lax.fori_loop(0, steps, finish, 0)


def shards(
    fine_latent, coarse_latent, parents, interp_weights, live_rows, w_fine, w_parent, w_edge_out,
    w_node_fine, w_node_agg, w_node_out, edge_bias, node_bias, norm_gain, norm_bias,
):
    fine_count = fine_latent.shape[1]
    block = coarse_latent.shape[1]
    mine = fine_count // OWNERS
    steps = mine // STEP
    pairs = [
        (PARTS,), (steps,), (OWNERS, PARTS), (OWNERS, steps), (3, 3, PARTS), (3, 4, PARTS),
        (2, PARTS), (steps,), (steps,), (OWNERS, steps), (steps,),
    ]
    updated, _, _ = pl.pallas_call(
        kernel,
        out_shape=(
            jax.ShapeDtypeStruct((SLICE, fine_count), BF16),
            jax.ShapeDtypeStruct((PARENTS, mine), jnp.int32),
            jax.ShapeDtypeStruct((PARENTS, mine), F32),
        ),
        in_specs=[ANY] * 4 + [VMEM] * 10,
        out_specs=(ANY, ANY, ANY),
        scratch_shapes=[
            pltpu.VMEM((SLICE, block), BF16),
            pltpu.VMEM((SLICE, fine_count), BF16),
            pltpu.VMEM((D, block // OWNERS), BF16),
            pltpu.VMEM((3 * block, 2, HALF), BF16),
            pltpu.VMEM((D, mine), BF16),
            pltpu.VMEM((D, mine), BF16),
            pltpu.VMEM((SLICE, fine_count), BF16),
            pltpu.VMEM((STEP, 2, HALF), F32),
            pltpu.VMEM((STEP, 2, HALF), F32),
            pltpu.SMEM((PARENTS, mine), jnp.int32),
            pltpu.SMEM((PARENTS, mine), F32),
        ] + [DMA(shape) for shape in pairs for _ in range(2)] + [DMA((PARTS + steps + 2,))],
        compiler_params=pltpu.CompilerParams(
            collective_id=0, has_side_effects=True, vmem_limit_bytes=VMEM_LIMIT
        ),
    )(
        coarse_latent, fine_latent, parents, interp_weights, w_parent, w_fine, w_edge_out,
        w_node_fine, w_node_agg, w_node_out, edge_bias[None], node_bias[None], norm_gain[None],
        norm_bias[None],
    )
    live = jnp.arange(fine_count, dtype=jnp.int32) < live_rows[0]
    return jnp.where(live[None, :], updated, fine_latent)


def solution(mesh):
    in_specs = (
        P("feat", "dom"), P("feat", "dom"), P(None, "dom"), P(None, "dom"), P("dom"),
        P(), P(), P(), P(), P(), P(), P(), P(), P(), P(),
    )
    return jax.shard_map(
        shards, mesh=mesh, in_specs=in_specs, out_specs=P("feat", "dom"), check_vma=False
    )
```
